32 devices in a mesh: user: 8 (over y, x, core), item: 4 (over z).
Axes of the slice: x: 2, y: 2, z: 4, core: 2. Of those that a mesh axis runs over, the one named last changes fastest.
Arguments:
- users: float32 [8192, 256], P(('user', 'item')), may hold values from -1.5 to 1.5
- user_accum: float32 [8192, 256], P(('user', 'item')), may hold values from 0.1 to 10
- items: float32 [8192, 256], P(('user', 'item')), may hold values from -1.5 to 1.5
- item_accum: float32 [8192, 256], P(('user', 'item')), may hold values from 0.1 to 10
- ratings: int32 [2, 8192, 1024], P(None, 'user', 'item'), may hold values from 0 to 1
- tile_mask: int32 [2, 64, 8], P(None, 'user', 'item'), may hold values 0 or 1
Outputs:
- users_out: float32 [8192, 256], P(('user', 'item'))
- items_out: float32 [8192, 256], P(('user', 'item'))
The draws below stay inside these ranges and needn't reach their ends.
All inputs are finite; a program needn't handle non-finite values. No bound on the sum of `tile_mask` on one device may be relied on, other than what follows from the above.
Results may differ from the reference program's by a relative error of at most 0.013.
Values may be sent and summed in bfloat16 or wider, within the bound.
No kernel may reach another device: no remote copies, remote signals or barrier semaphores. Data moves between devices by JAX's collectives and lax.ppermute only.
A program may use at most 64 MiB of HBM per device.

```python
import math
import jax
import jax.numpy as jnp
from jax import lax

R = 256
TILE = 128
STRATA = 2
USERS = 8192
BLK = 1024
ITEMS = 8192
N_USER = 8


def touch_ends(values, stream_key, least, top_value):
    place = [jax.random.randint(jax.random.fold_in(stream_key, axis), (), 0, length) for axis, length in enumerate(values.shape)]
    widest = values.shape.index(max(values.shape))
    neighbour = place[:widest] + [(place[widest] + 1) % values.shape[widest]] + place[widest + 1:]
    return values.at[tuple(place)].set(least).at[tuple(neighbour)].set(top_value)


def shard_levels(stream_key, dims, cuts, least, largest):
    def one(dim, shards_of):
        draws = jax.random.uniform(jax.random.fold_in(jax.random.fold_in(stream_key, 6), dim), (shards_of,), jnp.float32, least / len(cuts), largest / len(cuts))
        return jnp.repeat(jnp.exp(draws), dims[dim] // shards_of).reshape((-1,) + (1,) * (len(dims) - dim - 1))

    gain = one(*cuts[0])
    for cut in cuts[1:]:
        gain = gain * one(*cut)
    return gain


def bell_draw(rng, shape, deviation, reach, split=(), kind=jnp.bfloat16):
    array = jax.random.normal(rng, shape, jnp.float32) * deviation
    if len(split) > 0:
        array = shard_levels(rng, shape, split, -0.22, 0.18) * array
    return jnp.clip(array, min=-reach, max=reach).astype(kind)


def setup_inputs(seed: int = 0) -> dict:
    key_list = jax.random.split(jax.random.key(seed), 7)
    return {
        "users": bell_draw(key_list[0], (USERS, R), 0.25, 1.5, ((0, 32),), jnp.float32),
        "user_accum": jnp.clip(jnp.exp(math.log(10.0) - 4.6051702 * jax.random.uniform(key_list[1], (USERS, R), jnp.float32) ** shard_levels(key_list[1], (USERS, R), ((0, 32),), -0.2, 0.2)), 0.1, 10.0),
        "items": bell_draw(key_list[2], (ITEMS, R), 0.25, 1.5, ((0, 32),), jnp.float32),
        "item_accum": jnp.clip(jnp.exp(math.log(10.0) - 4.6051702 * jax.random.uniform(key_list[3], (ITEMS, R), jnp.float32) ** shard_levels(key_list[3], (ITEMS, R), ((0, 32),), -0.2, 0.2)), 0.1, 10.0),
        "ratings": touch_ends(jax.random.randint(key_list[4], (STRATA, USERS, BLK), 0, 2), jax.random.fold_in(key_list[4], 1), 0, 1).astype(jnp.int32),
        "tile_mask": touch_ends((jax.random.randint(key_list[5], (STRATA, USERS // TILE, BLK // TILE), 0, 5) < 3).astype(jnp.int32), jax.random.fold_in(key_list[5], 1), 0, 1),
    }


def adagrad(param, accum, grad):
    accum = accum + grad * grad
    return (param - 0.25 * grad / (jnp.sqrt(accum) + 1e-06), accum)

def expand_mask(mask, rows, cols):
    full = jnp.broadcast_to(mask.astype(jnp.float32)[:, None, :, None], (rows // TILE, TILE, cols // TILE, TILE))
    return full.reshape(rows, cols)

def one_block(packed):
    user_rows, user_acc, item_rows, item_acc, rates, mask = packed
    user_bf = user_rows.astype(jnp.bfloat16)
    item_bf = item_rows.astype(jnp.bfloat16)
    logits = lax.dot_general(user_bf, item_bf, (((1,), (1,)), ((), ())), preferred_element_type=jnp.float32)
    observed = expand_mask(mask, user_rows.shape[0], item_rows.shape[0])
    errors = (observed * (jax.nn.sigmoid(logits) - rates.astype(jnp.float32))).astype(jnp.bfloat16)
    user_grad = jnp.dot(errors, item_bf, preferred_element_type=jnp.float32) + 0.1 * user_rows
    item_grad = lax.dot_general(errors, user_bf, (((0,), (0,)), ((), ())), preferred_element_type=jnp.float32) + 0.1 * item_rows
    new_users, new_uacc = adagrad(user_rows, user_acc, user_grad)
    new_items, new_iacc = adagrad(item_rows, item_acc, item_grad)
    return (new_users, new_uacc, new_items, new_iacc)

def reference(users, user_accum, items, item_accum, ratings, tile_mask):
    block_users = users.shape[0] // N_USER
    block_items = items.shape[0] // N_USER
    rank = users.shape[1]
    for stratum in range(STRATA):
        ublocks = users.reshape(N_USER, block_users, rank)
        uacc = user_accum.reshape(N_USER, block_users, rank)
        iblocks = jnp.roll(items.reshape(N_USER, block_items, rank), stratum, axis=0)
        iacc = jnp.roll(item_accum.reshape(N_USER, block_items, rank), stratum, axis=0)
        rates = ratings[stratum].reshape(N_USER, block_users, block_items)
        masks = tile_mask[stratum].reshape(N_USER, block_users // TILE, block_items // TILE)
        new_u, new_ua, new_i, new_ia = lax.map(one_block, (ublocks, uacc, iblocks, iacc, rates, masks))
        users = new_u.reshape(-1, rank)
        user_accum = new_ua.reshape(-1, rank)
        items = jnp.roll(new_i, -stratum, axis=0).reshape(-1, rank)
        item_accum = jnp.roll(new_ia, -stratum, axis=0).reshape(-1, rank)
    return (users, items)
```

```python
import jax
import jax.numpy as jnp
from jax import lax
from jax.sharding import PartitionSpec as P

BF = jnp.bfloat16
F32 = jnp.float32


def adagrad(param, accum, grad):
    accum = accum + grad * grad
    return (param - 0.25 * grad / (jnp.sqrt(accum) + 1e-06), accum)


def move(array, by_user, item_map):
    n_user, n_item = lax.axis_size("user"), lax.axis_size("item")
    if by_user == 0:
        return lax.ppermute(array, "item", [(z, item_map(z)) for z in range(n_item)])
    pairs = [
        (u * n_item + z, (u + by_user) % n_user * n_item + item_map(z))
        for u in range(n_user)
        for z in range(n_item)
    ]
    return lax.ppermute(array, ("user", "item"), pairs)


def dot(a, b, ca, cb):
    return lax.dot_general(a, b, (((ca,), (cb,)), ((), ())), preferred_element_type=F32)


def body(users, user_accum, items, item_accum, ratings, tile_mask):
    strata, block_users, cols = ratings.shape
    rows, rank = users.shape
    n = lax.axis_size("item")
    z = lax.axis_index("item")
    group = n // 2
    side = block_users // tile_mask.shape[1]
    other = z ^ 1

    def shard(array, first, k):
        return lax.dynamic_slice_in_dim(array, lax.rem(first + 2 * k, n) * rows, rows, 0)

    wide = jnp.repeat(tile_mask, side, axis=2).astype(BF).reshape(-1, cols)
    first_items = items.astype(BF)
    both = move(jnp.concatenate((first_items, wide)), 0, lambda i: i ^ 1)
    mine_wide = wide.reshape(strata, -1, cols)
    other_wide = both[cols:].reshape(strata, -1, cols)

    def observed(masks, first, k):
        return shard(jnp.repeat(masks, side, axis=0), first, k)

    rates, seen = [], []
    for s in range(strata):
        sent = [shard(ratings[s], other, k).astype(BF) for k in range(group)]
        got = [move(t, 0, lambda i: i ^ 1) for t in sent]
        rates.append([
            jnp.concatenate((shard(ratings[s], z, k).astype(BF), got[k]), axis=1)
            for k in range(group)
        ])
        seen.append([
            jnp.concatenate((observed(mine_wide[s], z, k), observed(other_wide[s], z, k)), axis=1)
            for k in range(group)
        ])

    for s in range(strata):
        users_bf = users.astype(BF)
        shards = [users_bf] + [
            move(users_bf, 0, lambda i, k=k: (i - 2 * k) % n) for k in range(1, group)
        ]
        if s == 0:
            pair = jnp.concatenate((first_items, both[:cols]))
        else:
            items_bf = items.astype(BF)
            pair = jnp.concatenate(
                (move(items_bf, s, lambda i: i), move(items_bf, s, lambda i: i ^ 1))
            )
        user_grad = 0.1 * users
        item_part = 0.0
        for k in reversed(range(group)):
            logits = dot(shards[k], pair, 1, 1)
            errors = (
                seen[s][k].astype(F32) * (jax.nn.sigmoid(logits) - rates[s][k].astype(F32))
            ).astype(BF)
            part = dot(errors, pair, 1, 0)
            if k:
                part = move(part.astype(BF), 0, lambda i: (i + 2 * k) % n).astype(F32)
            user_grad = user_grad + part
            item_part = item_part + dot(errors, shards[k], 0, 0)
        near, far = item_part[:cols], item_part[cols:].astype(BF)
        if s:
            near = move(near.astype(BF), -s, lambda i: i).astype(F32)
        far = move(far, -s, lambda i: i ^ 1).astype(F32)
        item_grad = near + far + 0.1 * items
        users, user_accum = adagrad(users, user_accum, user_grad)
        items, item_accum = adagrad(items, item_accum, item_grad)
    return (users, items)


def solution(mesh):
    rows = P(("user", "item"), None)
    blocks = P(None, "user", "item")
    return jax.shard_map(
        body,
        mesh=mesh,
        in_specs=(rows, rows, rows, rows, blocks, blocks),
        out_specs=(rows, rows),
        check_vma=False,
    )
```

```python
import functools

import jax
import jax.numpy as jnp
from jax import lax
from jax.experimental import pallas as pl
from jax.experimental.pallas import tpu as pltpu
from jax.sharding import PartitionSpec as P


BF = jnp.bfloat16
F32 = jnp.float32
FIRST_PARAMS = pltpu.CompilerParams(vmem_limit_bytes=16<<20)
REST_PARAMS = pltpu.CompilerParams(vmem_limit_bytes=16 << 20)


def adagrad(param, accum, grad):
    accum = accum + grad * grad
    return (param - 0.25 * grad / (jnp.sqrt(accum) + 1e-06), accum)


def move(array, by_user, item_map):
    n_user, n_item = lax.axis_size("user"), lax.axis_size("item")
    if by_user == 0:
        return lax.ppermute(array, "item", [(z, item_map(z)) for z in range(n_item)])
    pairs = [
        (u * n_item + z, (u + by_user) % n_user * n_item + item_map(z))
        for u in range(n_user)
        for z in range(n_item)
    ]
    return lax.ppermute(array, ("user", "item"), pairs)


def dot(a, b, ca, cb):
    return lax.dot_general(a, b, (((ca,), (cb,)), ((), ())), preferred_element_type=F32)


def shard_kernel(k, first_tile, side, carried, *refs):
    if carried:
        u, near, far, rate_near, rate_far, seen_near, seen_far, near_in, far_in = refs[:9]
    else:
        u, near, far, rate_near, rate_far, seen_near, seen_far = refs[:7]
    part, near_out, far_out = refs[-3:]
    rows = u.shape[0]
    shard = lax.rem(lax.axis_index("item") + 2 * k, lax.axis_size("item"))
    chunk = min(rows, side)

    def errors(items, rates, seen):
        tiles, cols = seen.shape
        masks = seen[...].astype(F32)
        at = lax.broadcasted_iota(jnp.int32, (tiles, cols), 0)
        bands = []
        for t in range(0, rows, chunk):
            tile = first_tile + (shard * rows + t) // side
            row = jnp.sum(jnp.where(at == tile, masks, 0.0), axis=0, keepdims=True)
            bands.append(jnp.broadcast_to(row, (chunk, cols)))
        observed = jnp.concatenate(bands, axis=0) if len(bands) > 1 else bands[0]
        logits = dot(u[...], items[...], 1, 1)
        return (observed * (jax.nn.sigmoid(logits) - rates[...].astype(F32))).astype(BF)

    e_near = errors(near, rate_near, seen_near)
    e_far = errors(far, rate_far, seen_far)
    part[...] = (dot(e_near, near[...], 1, 0) + dot(e_far, far[...], 1, 0)).astype(part.dtype)
    g_near = dot(e_near, u[...], 0, 0)
    g_far = dot(e_far, u[...], 0, 0)
    if carried:
        g_near = g_near + near_in[...]
        g_far = g_far + far_in[...]
    near_out[...] = g_near.astype(near_out.dtype)
    far_out[...] = g_far.astype(far_out.dtype)


def shard_grads(k, first_tile, side, part_type, item_types, args, carry):
    u, near = args[0], args[1]
    rows, rank = u.shape
    cols = near.shape[0]
    spec = pl.BlockSpec(memory_space=pltpu.VMEM)
    operands = args + carry
    return pl.pallas_call(
        functools.partial(shard_kernel, k, first_tile, side, bool(carry)),
        out_shape=(
            jax.ShapeDtypeStruct((rows, rank), part_type),
            jax.ShapeDtypeStruct((cols, rank), item_types[0]),
            jax.ShapeDtypeStruct((cols, rank), item_types[1]),
        ),
        in_specs=[spec] * len(operands),
        out_specs=(spec,) * 3,
        compiler_params=pltpu.CompilerParams(vmem_limit_bytes=16 << 20),
        cost_estimate=pl.CostEstimate(
            flops=12 * rows * cols * rank, bytes_accessed=0, transcendentals=2 * rows * cols
        ),
        name="shard_grads",
    )(*operands)


def fetch(sources, buffers, sems):
    copies = [
        pltpu.make_async_copy(src, buf, sems.at[i])
        for i, (src, buf) in enumerate(zip(sources, buffers))
    ]
    for copy in copies:
        copy.start()
    return copies


def share(ratings, s, first, k, rows, n):
    at = pl.multiple_of(lax.rem(first + 2 * k, n) * rows, rows)
    return ratings.at[s, pl.ds(at, rows), :]


def first_kernel(group, rows, side, *refs):
    users, items, ratings, masks = refs[:4]
    users_bf, items_bf, wide = refs[4:7]
    sent = refs[7 : 7 + group]
    scratch = refs[7 + group :]
    sems = scratch[-1]
    n = lax.axis_size("item")
    other = lax.axis_index("item") ^ 1
    order = list(range(1, group)) + [0]
    sources = [items, users, masks] + [share(ratings, 0, other, k, rows, n) for k in order]
    copies = fetch(sources, scratch[:-1], sems)
    for i, out in enumerate((items_bf, users_bf)):
        copies[i].wait()
        out[...] = scratch[i][...].astype(BF)
    copies[2].wait()
    strata, across, tiles = masks.shape
    eye = lax.broadcasted_iota(jnp.int32, (tiles, tiles), 0) == lax.broadcasted_iota(
        jnp.int32, (tiles, tiles), 1
    )
    for s in range(strata):
        band = scratch[2][s].astype(F32)
        parts = []
        for c in range(across):
            spread = jnp.where(eye, jnp.broadcast_to(band[c : c + 1], (tiles, tiles)), 0.0)
            parts.append(jnp.broadcast_to(jnp.sum(spread, axis=1, keepdims=True), (tiles, side)))
        wide[pl.ds(s * tiles, tiles), :] = jnp.concatenate(parts, axis=1)
    for i, out in enumerate(sent):
        copies[3 + i].wait()
        out[pl.ds(0, rows), :] = scratch[3 + i][...].astype(F32).astype(BF)
    sent[0][pl.ds(rows, strata * tiles), :] = wide[...].astype(BF)


def first_sends(users, items, ratings, tile_mask, group, side):
    rows, _ = users.shape
    cols = ratings.shape[2]
    masks = tile_mask.transpose(0, 2, 1)
    wide = (tile_mask.shape[0] * tile_mask.shape[1], cols)
    vmem = pl.BlockSpec(memory_space=pltpu.VMEM)
    out_shape = [
        jax.ShapeDtypeStruct(users.shape, BF),
        jax.ShapeDtypeStruct(items.shape, BF),
        jax.ShapeDtypeStruct(wide, F32),
        jax.ShapeDtypeStruct((rows + wide[0], cols), BF),
    ] + [jax.ShapeDtypeStruct((rows, cols), BF)] * (group - 1)
    return pl.pallas_call(
        functools.partial(first_kernel, group, rows, side),
        out_shape=tuple(out_shape),
        in_specs=[pl.BlockSpec(memory_space=pltpu.HBM)] * 4,
        out_specs=(vmem,) * len(out_shape),
        scratch_shapes=[
            pltpu.VMEM(items.shape, F32),
            pltpu.VMEM(users.shape, F32),
            pltpu.VMEM(masks.shape, jnp.int32),
        ]
        + [pltpu.VMEM((rows, cols), jnp.int32)] * group
        + [pltpu.SemaphoreType.DMA((3 + group,))],
        compiler_params=FIRST_PARAMS,
        name="first_sends",
    )(*(pltpu.with_memory_space_constraint(a, pltpu.HBM) for a in (users, items, ratings, masks)))


def rest_kernel(picks, rows, ratings, *refs):
    outs, bufs, sems = refs[: len(picks)], refs[len(picks) : -1], refs[-1]
    n = lax.axis_size("item")
    z = lax.axis_index("item")
    copies = fetch(
        [share(ratings, s, z ^ 1 if away else z, k, rows, n) for s, k, away in picks], bufs, sems
    )
    for copy, buf, out in zip(copies, bufs, outs):
        copy.wait()
        out[...] = buf[...].astype(F32).astype(BF)


def rest_of_ratings(ratings, picks, rows):
    cols = ratings.shape[2]
    vmem = pl.BlockSpec(memory_space=pltpu.VMEM)
    return pl.pallas_call(
        functools.partial(rest_kernel, picks, rows),
        out_shape=(jax.ShapeDtypeStruct((rows, cols), BF),) * len(picks),
        in_specs=[pl.BlockSpec(memory_space=pltpu.HBM)],
        out_specs=(vmem,) * len(picks),
        scratch_shapes=[pltpu.VMEM((rows, cols), jnp.int32)] * len(picks)
        + [pltpu.SemaphoreType.DMA((len(picks),))],
        compiler_params=REST_PARAMS,
        name="rest_of_ratings",
    )(ratings)


def body(users, user_accum, items, item_accum, ratings, tile_mask):
    strata, block_users, _ = ratings.shape
    rows, _ = users.shape
    n = lax.axis_size("item")
    group = n // 2
    tiles = tile_mask.shape[1]
    side = block_users // tiles
    order = list(range(1, group)) + [0]

    first_users, first_items, wide, *sends = first_sends(
        users, items, ratings, tile_mask, group, side
    )
    shards = {0: first_users}
    for k in range(1, group):
        shards[k] = move(first_users, 0, lambda i: (i - 2 * k) % n)
    near, far = first_items, move(first_items, 0, lambda i: i ^ 1)

    picks = [(s, k, True) for s in range(1, strata) for k in order]
    picks += [(s, k, False) for s in range(strata) for k in order]
    rest = dict(zip(picks, rest_of_ratings(ratings, picks, rows)))
    rest.update({(0, k, True): t for k, t in zip(order, sends)})
    rates = {}
    for s in range(strata):
        for k in order:
            got = move(rest[s, k, True], 0, lambda i: i ^ 1)
            if s == 0 and k == order[0]:
                got, far_wide = got[:rows], got[rows:]
            rates[s, k] = (rest[s, k, False], got)

    for s in range(strata):
        if s:
            users_bf = users.astype(BF)
            shards = {0: users_bf}
            for k in range(1, group):
                shards[k] = move(users_bf, 0, lambda i: (i - 2 * k) % n)
            items_bf = items.astype(BF)
            near = move(items_bf, s, lambda i: i)
            far = move(items_bf, s, lambda i: i ^ 1)
        user_grad = 0.1 * users
        carry = ()
        turn = order
        for k in turn:
            last = k == turn[-1]
            part, g_near, g_far = shard_grads(
                k,
                s * tiles,
                side,
                BF if k else F32,
                (BF if last and s else F32, BF if last else F32),
                (shards[k], near, far, *rates[s, k], wide, far_wide),
                carry,
            )
            carry = (g_near, g_far)
            if k:
                part = move(part, 0, lambda i: (i + 2 * k) % n).astype(F32)
            user_grad = user_grad + part
        g_near, g_far = carry
        if s:
            g_near = move(g_near, -s, lambda i: i).astype(F32)
        g_far = move(g_far, -s, lambda i: i ^ 1).astype(F32)
        item_grad = g_near + g_far + 0.1 * items
        users, user_accum = adagrad(users, user_accum, user_grad)
        items, item_accum = adagrad(items, item_accum, item_grad)
    return (users, items)


def solution(mesh):
    rows = P(("user", "item"), None)
    blocks = P(None, "user", "item")

    return jax.shard_map(
        body,
        mesh=mesh,
        in_specs=(rows, rows, rows, rows, blocks, blocks),
        out_specs=(rows, rows),
        check_vma=False,
    )
```

```python
import functools

import jax
import jax.numpy as jnp
from jax import lax
from jax.experimental import pallas as pl
from jax.experimental.pallas import tpu as pltpu
from jax.sharding import PartitionSpec as P


BF = jnp.bfloat16
F32 = jnp.float32
SMALL = pltpu.CompilerParams(vmem_limit_bytes=16 << 20)


def adagrad(param, accum, grad):
    accum = accum + grad * grad
    return (param - 0.25 * grad / (jnp.sqrt(accum) + 1e-06), accum)


def move(array, by_user, item_map):
    n_user, n_item = lax.axis_size("user"), lax.axis_size("item")
    if by_user == 0:
        return lax.ppermute(array, "item", [(z, item_map(z)) for z in range(n_item)])
    pairs = [
        (u * n_item + z, (u + by_user) % n_user * n_item + item_map(z))
        for u in range(n_user)
        for z in range(n_item)
    ]
    return lax.ppermute(array, ("user", "item"), pairs)


def dot(a, b, ca, cb):
    return lax.dot_general(a, b, (((ca,), (cb,)), ((), ())), preferred_element_type=F32)


def shard_kernel(k, first_tile, side, carried, *refs):
    if carried:
        u, near, far, rate_near, rate_far, seen_near, seen_far, near_in, far_in = refs[:9]
    else:
        u, near, far, rate_near, rate_far, seen_near, seen_far = refs[:7]
    part, near_out, far_out = refs[-3:]
    rows = u.shape[0]
    shard = lax.rem(lax.axis_index("item") + 2 * k, lax.axis_size("item"))
    chunk = min(rows, side)

    def errors(items, rates, seen):
        tiles, cols = seen.shape
        masks = seen[...].astype(F32)
        at = lax.broadcasted_iota(jnp.int32, (tiles, cols), 0)
        bands = []
        for t in range(0, rows, chunk):
            tile = first_tile + (shard * rows + t) // side
            row = jnp.sum(jnp.where(at == tile, masks, 0.0), axis=0, keepdims=True)
            bands.append(jnp.broadcast_to(row, (chunk, cols)))
        observed = jnp.concatenate(bands, axis=0) if len(bands) > 1 else bands[0]
        logits = dot(u[...], items[...], 1, 1)
        return (observed * (jax.nn.sigmoid(logits) - rates[...].astype(F32))).astype(BF)

    e_near = errors(near, rate_near, seen_near)
    e_far = errors(far, rate_far, seen_far)
    part[...] = (dot(e_near, near[...], 1, 0) + dot(e_far, far[...], 1, 0)).astype(part.dtype)
    g_near = dot(e_near, u[...], 0, 0)
    g_far = dot(e_far, u[...], 0, 0)
    if carried:
        g_near = g_near + near_in[...]
        g_far = g_far + far_in[...]
    near_out[...] = g_near.astype(near_out.dtype)
    far_out[...] = g_far.astype(far_out.dtype)


def shard_grads(k, first_tile, side, part_type, item_types, args, carry):
    u, near = args[0], args[1]
    rows, rank = u.shape
    cols = near.shape[0]
    spec = pl.BlockSpec(memory_space=pltpu.VMEM)
    operands = args + carry
    return pl.pallas_call(
        functools.partial(shard_kernel, k, first_tile, side, bool(carry)),
        out_shape=(
            jax.ShapeDtypeStruct((rows, rank), part_type),
            jax.ShapeDtypeStruct((cols, rank), item_types[0]),
            jax.ShapeDtypeStruct((cols, rank), item_types[1]),
        ),
        in_specs=[spec] * len(operands),
        out_specs=(spec,) * 3,
        compiler_params=SMALL,
        cost_estimate=pl.CostEstimate(
            flops=12 * rows * cols * rank, bytes_accessed=0, transcendentals=2 * rows * cols
        ),
        name="shard_grads",
    )(*operands)


def fetch(sources, buffers, sems):
    copies = [
        pltpu.make_async_copy(src, buf, sems.at[i])
        for i, (src, buf) in enumerate(zip(sources, buffers))
    ]
    for copy in copies:
        copy.start()
    return copies


def share(ratings, s, first, k, rows, n):
    at = pl.multiple_of(lax.rem(first + 2 * k, n) * rows, rows)
    return ratings.at[s, pl.ds(at, rows), :]


def rows_kernel(*refs):
    count = (len(refs) - 1) // 3
    sources, outs, bufs, sems = refs[:count], refs[count : 2 * count], refs[2 * count : -1], refs[-1]
    for copy, buf, out in zip(fetch(sources, bufs, sems), bufs, outs):
        copy.wait()
        out[...] = buf[...].astype(BF)


def first_rows(*arrays):
    return pl.pallas_call(
        rows_kernel,
        out_shape=tuple(jax.ShapeDtypeStruct(a.shape, BF) for a in arrays),
        in_specs=[pl.BlockSpec(memory_space=pltpu.HBM)] * len(arrays),
        out_specs=(pl.BlockSpec(memory_space=pltpu.VMEM),) * len(arrays),
        scratch_shapes=[pltpu.VMEM(a.shape, a.dtype) for a in arrays]
        + [pltpu.SemaphoreType.DMA((len(arrays),))],
        compiler_params=SMALL,
        name="first_rows",
    )(*(pltpu.with_memory_space_constraint(a, pltpu.HBM) for a in arrays))


def first_kernel(group, rows, side, *refs):
    ratings, masks, wide = refs[:3]
    sent = refs[3 : 3 + group]
    scratch = refs[3 + group :]
    n = lax.axis_size("item")
    other = lax.axis_index("item") ^ 1
    order = list(range(1, group)) + [0]
    sources = [masks] + [share(ratings, 0, other, k, rows, n) for k in order]
    copies = fetch(sources, scratch[:-1], scratch[-1])
    copies[0].wait()
    strata, across, tiles = masks.shape
    eye = lax.broadcasted_iota(jnp.int32, (tiles, tiles), 0) == lax.broadcasted_iota(
        jnp.int32, (tiles, tiles), 1
    )
    for s in range(strata):
        band = scratch[0][s].astype(F32)
        parts = []
        for c in range(across):
            spread = jnp.where(eye, jnp.broadcast_to(band[c : c + 1], (tiles, tiles)), 0.0)
            parts.append(jnp.broadcast_to(jnp.sum(spread, axis=1, keepdims=True), (tiles, side)))
        wide[pl.ds(s * tiles, tiles), :] = jnp.concatenate(parts, axis=1)
    for i, out in enumerate(sent):
        copies[1 + i].wait()
        out[pl.ds(0, rows), :] = scratch[1 + i][...].astype(F32).astype(BF)
    sent[0][pl.ds(rows, strata * tiles), :] = wide[...].astype(BF)


def first_sends(ratings, tile_mask, rows, group, side):
    cols = ratings.shape[2]
    masks = tile_mask.transpose(0, 2, 1)
    wide = (tile_mask.shape[0] * tile_mask.shape[1], cols)
    vmem = pl.BlockSpec(memory_space=pltpu.VMEM)
    out_shape = [
        jax.ShapeDtypeStruct(wide, F32),
        jax.ShapeDtypeStruct((rows + wide[0], cols), BF),
    ] + [jax.ShapeDtypeStruct((rows, cols), BF)] * (group - 1)
    return pl.pallas_call(
        functools.partial(first_kernel, group, rows, side),
        out_shape=tuple(out_shape),
        in_specs=[pl.BlockSpec(memory_space=pltpu.HBM)] * 2,
        out_specs=(vmem,) * len(out_shape),
        scratch_shapes=[pltpu.VMEM(masks.shape, jnp.int32)]
        + [pltpu.VMEM((rows, cols), jnp.int32)] * group
        + [pltpu.SemaphoreType.DMA((1 + group,))],
        compiler_params=SMALL,
        name="first_sends",
    )(*(pltpu.with_memory_space_constraint(a, pltpu.HBM) for a in (ratings, masks)))


def rest_kernel(picks, rows, ratings, *refs):
    outs, bufs, sems = refs[: len(picks)], refs[len(picks) : -1], refs[-1]
    n = lax.axis_size("item")
    z = lax.axis_index("item")
    copies = fetch(
        [share(ratings, s, z ^ 1 if away else z, k, rows, n) for s, k, away in picks], bufs, sems
    )
    for copy, buf, out in zip(copies, bufs, outs):
        copy.wait()
        out[...] = buf[...].astype(F32).astype(BF)


def rest_of_ratings(ratings, picks, rows):
    cols = ratings.shape[2]
    vmem = pl.BlockSpec(memory_space=pltpu.VMEM)
    return pl.pallas_call(
        functools.partial(rest_kernel, picks, rows),
        out_shape=(jax.ShapeDtypeStruct((rows, cols), BF),) * len(picks),
        in_specs=[pl.BlockSpec(memory_space=pltpu.HBM)],
        out_specs=(vmem,) * len(picks),
        scratch_shapes=[pltpu.VMEM((rows, cols), jnp.int32)] * len(picks)
        + [pltpu.SemaphoreType.DMA((len(picks),))],
        compiler_params=SMALL,
        name="rest_of_ratings",
    )(pltpu.with_memory_space_constraint(ratings, pltpu.HBM))


def last_kernel(count, *refs):
    param, accum = refs[:2]
    grads, out, buf, sems = refs[2:-3], refs[-3], refs[-2], refs[-1]
    band = param.shape[0] // count
    copies = []
    for i in range(count):
        here = pl.ds(i * band, band)
        old = param[here, :]
        grad = 0.1 * old
        for share in grads:
            grad = grad + share[here, :].astype(F32)
        buf[here, :] = adagrad(old, accum[here, :], grad)[0]
        copies.append(pltpu.make_async_copy(buf.at[here, :], out.at[here, :], sems.at[i]))
        copies[-1].start()
    for copy in copies:
        copy.wait()


def last_update(param, accum, *grads):
    count = 4
    vmem = pl.BlockSpec(memory_space=pltpu.VMEM)
    return pl.pallas_call(
        functools.partial(last_kernel, count),
        out_shape=jax.ShapeDtypeStruct(param.shape, F32),
        in_specs=[vmem] * (2 + len(grads)),
        out_specs=pl.BlockSpec(memory_space=pltpu.HBM),
        scratch_shapes=[pltpu.VMEM(param.shape, F32), pltpu.SemaphoreType.DMA((count,))],
        compiler_params=SMALL,
        name="last_update",
    )(param, accum, *grads)


def body(users, user_accum, items, item_accum, ratings, tile_mask):
    strata, block_users, _ = ratings.shape
    rows, _ = users.shape
    n = lax.axis_size("item")
    group = n // 2
    tiles = tile_mask.shape[1]
    side = block_users // tiles
    order = list(range(1, group)) + [0]

    first_items, first_users = first_rows(items, users)
    wide, *sends = first_sends(ratings, tile_mask, rows, group, side)
    shards = {0: first_users}
    for k in range(1, group):
        shards[k] = move(first_users, 0, lambda i: (i - 2 * k) % n)
    near, far = first_items, move(first_items, 0, lambda i: i ^ 1)

    picks = [(s, k, True) for s in range(1, strata) for k in order]
    picks += [(s, k, False) for s in range(strata) for k in order]
    rest = dict(zip(picks, rest_of_ratings(ratings, picks, rows)))
    rest.update({(0, k, True): t for k, t in zip(order, sends)})
    rates = {}
    for s in range(strata):
        for k in order:
            got = move(rest[s, k, True], 0, lambda i: i ^ 1)
            if s == 0 and k == order[0]:
                got, far_wide = got[:rows], got[rows:]
            rates[s, k] = (rest[s, k, False], got)

    for s in range(strata):
        if s:
            users_bf = users.astype(BF)
            shards = {0: users_bf}
            for k in range(1, group):
                shards[k] = move(users_bf, 0, lambda i: (i - 2 * k) % n)
            items_bf = items.astype(BF)
            near = move(items_bf, s, lambda i: i)
            far = move(items_bf, s, lambda i: i ^ 1)
        user_shares = []
        carry = ()
        for k in order:
            last = k == order[-1]
            part, g_near, g_far = shard_grads(
                k,
                s * tiles,
                side,
                BF if k else F32,
                (BF if last and s else F32, BF if last else F32),
                (shards[k], near, far, *rates[s, k], wide, far_wide),
                carry,
            )
            carry = (g_near, g_far)
            if k:
                part = move(part, 0, lambda i: (i + 2 * k) % n)
            user_shares.append(part)
        g_near, g_far = carry
        if s:
            g_near = move(g_near, -s, lambda i: i)
        g_far = move(g_far, -s, lambda i: i ^ 1)
        if s == strata - 1:
            users = last_update(users, user_accum, *user_shares)
            items = last_update(items, item_accum, g_near, g_far)
        else:
            user_grad = sum((t.astype(F32) for t in user_shares), 0.1 * users)
            item_grad = sum((t.astype(F32) for t in (g_near, g_far)), 0.1 * items)
            users, user_accum = adagrad(users, user_accum, user_grad)
            items, item_accum = adagrad(items, item_accum, item_grad)
    return (users, items)


def solution(mesh):
    rows = P(("user", "item"), None)
    blocks = P(None, "user", "item")

    return jax.shard_map(
        body,
        mesh=mesh,
        in_specs=(rows, rows, rows, rows, blocks, blocks),
        out_specs=(rows, rows),
        check_vma=False,
    )
```

```python
import functools

import jax
import jax.numpy as jnp
from jax import lax
from jax.experimental import pallas as pl
from jax.experimental.pallas import tpu as pltpu
from jax.sharding import PartitionSpec as P


BF = jnp.bfloat16
F32 = jnp.float32
SMALL = pltpu.CompilerParams(vmem_limit_bytes=16 << 20)


def adagrad(param, accum, grad):
    accum = accum + grad * grad
    return (param - 0.25 * grad / (jnp.sqrt(accum) + 1e-06), accum)


def move(array, by_user, item_map):
    n_user, n_item = lax.axis_size("user"), lax.axis_size("item")
    if by_user == 0:
        return lax.ppermute(array, "item", [(z, item_map(z)) for z in range(n_item)])
    pairs = [
        (u * n_item + z, (u + by_user) % n_user * n_item + item_map(z))
        for u in range(n_user)
        for z in range(n_item)
    ]
    return lax.ppermute(array, ("user", "item"), pairs)


def dot(a, b, ca, cb):
    return lax.dot_general(a, b, (((ca,), (cb,)), ((), ())), preferred_element_type=F32)


def tile_errors(k, first_tile, side, u, items, rates, seen):
    rows = u.shape[0]
    shard = lax.rem(lax.axis_index("item") + 2 * k, lax.axis_size("item"))
    chunk = min(rows, side)
    tiles, cols = seen.shape
    masks = seen[...].astype(F32)
    at = lax.broadcasted_iota(jnp.int32, (tiles, cols), 0)
    out = []
    for t in range(0, rows, chunk):
        tile = first_tile + (shard * rows + t) // side
        row = jnp.sum(jnp.where(at == tile, masks, 0.0), axis=0, keepdims=True)
        here = pl.ds(t, chunk)
        logits = dot(u[here, :], items[...], 1, 1)
        out.append((row * (jax.nn.sigmoid(logits) - rates[here, :].astype(F32))).astype(BF))
    return jnp.concatenate(out, axis=0) if len(out) > 1 else out[0]


def near_kernel(group, first_tile, side, *refs):
    shards, rates = refs[:group], refs[group : 2 * group]
    near, seen = refs[2 * group : 2 * group + 2]
    parts, grad = refs[2 * group + 2 : -1], refs[-1]
    total = None
    for k in range(group):
        errors = tile_errors(k, first_tile, side, shards[k], near, rates[k], seen)
        parts[k][...] = dot(errors, near[...], 1, 0)
        share = dot(errors, shards[k][...], 0, 0)
        total = share if total is None else total + share
    grad[...] = total.astype(grad.dtype)


def far_kernel(k, first_tile, side, *refs):
    u, far, rates, seen, part_in = refs[:5]
    carried, (part, grad) = refs[5:-2], refs[-2:]
    errors = tile_errors(k, first_tile, side, u, far, rates, seen)
    part[...] = (part_in[...] + dot(errors, far[...], 1, 0)).astype(part.dtype)
    share = dot(errors, u[...], 0, 0)
    for before in carried:
        share = share + before[...]
    grad[...] = share.astype(grad.dtype)


def tile_call(kernel, tiles, operands, out_shape):
    rows, rank = operands[0].shape
    cols = out_shape[-1].shape[0]
    spec = pl.BlockSpec(memory_space=pltpu.VMEM)
    return pl.pallas_call(
        kernel,
        out_shape=out_shape,
        in_specs=[spec] * len(operands),
        out_specs=(spec,) * len(out_shape),
        compiler_params=SMALL,
        cost_estimate=pl.CostEstimate(
            flops=6 * tiles * rows * cols * rank,
            bytes_accessed=0,
            transcendentals=2 * tiles * rows * cols,
        ),
    )(*operands)


def fetch(sources, buffers, sems):
    copies = [
        pltpu.make_async_copy(src, buf, sems.at[i])
        for i, (src, buf) in enumerate(zip(sources, buffers))
    ]
    for copy in copies:
        copy.start()
    return copies


def share(ratings, s, first, k, rows, n):
    at = pl.multiple_of(lax.rem(first + 2 * k, n) * rows, rows)
    return ratings.at[s, pl.ds(at, rows), :]


def rows_kernel(*refs):
    count = (len(refs) - 1) // 3
    sources, outs, bufs, sems = refs[:count], refs[count : 2 * count], refs[2 * count : -1], refs[-1]
    for copy, buf, out in zip(fetch(sources, bufs, sems), bufs, outs):
        copy.wait()
        out[...] = buf[...].astype(BF)


def first_rows(*arrays):
    return pl.pallas_call(
        rows_kernel,
        out_shape=tuple(jax.ShapeDtypeStruct(a.shape, BF) for a in arrays),
        in_specs=[pl.BlockSpec(memory_space=pltpu.HBM)] * len(arrays),
        out_specs=(pl.BlockSpec(memory_space=pltpu.VMEM),) * len(arrays),
        scratch_shapes=[pltpu.VMEM(a.shape, a.dtype) for a in arrays]
        + [pltpu.SemaphoreType.DMA((len(arrays),))],
        compiler_params=SMALL,
        name="first_rows",
    )(*(pltpu.with_memory_space_constraint(a, pltpu.HBM) for a in arrays))


def first_kernel(group, rows, side, *refs):
    ratings, masks, wide = refs[:3]
    sent = refs[3 : 3 + group]
    scratch = refs[3 + group :]
    n = lax.axis_size("item")
    other = lax.axis_index("item") ^ 1
    order = list(range(1, group)) + [0]
    sources = [masks] + [share(ratings, 0, other, k, rows, n) for k in order]
    copies = fetch(sources, scratch[:-1], scratch[-1])
    copies[0].wait()
    strata, across, tiles = masks.shape
    eye = lax.broadcasted_iota(jnp.int32, (tiles, tiles), 0) == lax.broadcasted_iota(
        jnp.int32, (tiles, tiles), 1
    )
    for s in range(strata):
        band = scratch[0][s].astype(F32)
        parts = []
        for c in range(across):
            spread = jnp.where(eye, jnp.broadcast_to(band[c : c + 1], (tiles, tiles)), 0.0)
            parts.append(jnp.broadcast_to(jnp.sum(spread, axis=1, keepdims=True), (tiles, side)))
        wide[pl.ds(s * tiles, tiles), :] = jnp.concatenate(parts, axis=1)
    for i, out in enumerate(sent):
        copies[1 + i].wait()
        out[pl.ds(0, rows), :] = scratch[1 + i][...].astype(F32).astype(BF)
    sent[0][pl.ds(rows, strata * tiles), :] = wide[...].astype(BF)


def first_sends(ratings, tile_mask, rows, group, side):
    cols = ratings.shape[2]
    masks = tile_mask.transpose(0, 2, 1)
    wide = (tile_mask.shape[0] * tile_mask.shape[1], cols)
    vmem = pl.BlockSpec(memory_space=pltpu.VMEM)
    out_shape = [
        jax.ShapeDtypeStruct(wide, F32),
        jax.ShapeDtypeStruct((rows + wide[0], cols), BF),
    ] + [jax.ShapeDtypeStruct((rows, cols), BF)] * (group - 1)
    return pl.pallas_call(
        functools.partial(first_kernel, group, rows, side),
        out_shape=tuple(out_shape),
        in_specs=[pl.BlockSpec(memory_space=pltpu.HBM)] * 2,
        out_specs=(vmem,) * len(out_shape),
        scratch_shapes=[pltpu.VMEM(masks.shape, jnp.int32)]
        + [pltpu.VMEM((rows, cols), jnp.int32)] * group
        + [pltpu.SemaphoreType.DMA((1 + group,))],
        compiler_params=SMALL,
        name="first_sends",
    )(*(pltpu.with_memory_space_constraint(a, pltpu.HBM) for a in (ratings, masks)))


def rest_kernel(picks, rows, ratings, *refs):
    outs, bufs, sems = refs[: len(picks)], refs[len(picks) : -1], refs[-1]
    n = lax.axis_size("item")
    z = lax.axis_index("item")
    copies = fetch(
        [share(ratings, s, z ^ 1 if away else z, k, rows, n) for s, k, away in picks], bufs, sems
    )
    for copy, buf, out in zip(copies, bufs, outs):
        copy.wait()
        out[...] = buf[...].astype(F32).astype(BF)


def rest_of_ratings(ratings, picks, rows):
    cols = ratings.shape[2]
    vmem = pl.BlockSpec(memory_space=pltpu.VMEM)
    return pl.pallas_call(
        functools.partial(rest_kernel, picks, rows),
        out_shape=(jax.ShapeDtypeStruct((rows, cols), BF),) * len(picks),
        in_specs=[pl.BlockSpec(memory_space=pltpu.HBM)],
        out_specs=(vmem,) * len(picks),
        scratch_shapes=[pltpu.VMEM((rows, cols), jnp.int32)] * len(picks)
        + [pltpu.SemaphoreType.DMA((len(picks),))],
        compiler_params=SMALL,
        name="rest_of_ratings",
    )(pltpu.with_memory_space_constraint(ratings, pltpu.HBM))


def last_kernel(count, *refs):
    param, accum = refs[:2]
    grads, out, buf, sems = refs[2:-3], refs[-3], refs[-2], refs[-1]
    band = param.shape[0] // count
    copies = []
    for i in range(count):
        here = pl.ds(i * band, band)
        old = param[here, :]
        grad = 0.1 * old
        for share in grads:
            grad = grad + share[here, :].astype(F32)
        buf[here, :] = adagrad(old, accum[here, :], grad)[0]
        copies.append(pltpu.make_async_copy(buf.at[here, :], out.at[here, :], sems.at[i]))
        copies[-1].start()
    for copy in copies:
        copy.wait()


def last_update(param, accum, *grads):
    count = 4
    vmem = pl.BlockSpec(memory_space=pltpu.VMEM)
    return pl.pallas_call(
        functools.partial(last_kernel, count),
        out_shape=jax.ShapeDtypeStruct(param.shape, F32),
        in_specs=[vmem] * (2 + len(grads)),
        out_specs=pl.BlockSpec(memory_space=pltpu.HBM),
        scratch_shapes=[pltpu.VMEM(param.shape, F32), pltpu.SemaphoreType.DMA((count,))],
        compiler_params=SMALL,
        name="last_update",
    )(param, accum, *grads)


def body(users, user_accum, items, item_accum, ratings, tile_mask):
    strata, block_users, cols = ratings.shape
    rows, rank = users.shape
    n = lax.axis_size("item")
    group = n // 2
    tiles = tile_mask.shape[1]
    side = block_users // tiles
    order = list(range(1, group)) + [0]

    first_items, first_users = first_rows(items, users)
    wide, *sends = first_sends(ratings, tile_mask, rows, group, side)
    shards = {0: first_users}
    for k in range(1, group):
        shards[k] = move(first_users, 0, lambda i: (i - 2 * k) % n)
    near, far = first_items, move(first_items, 0, lambda i: i ^ 1)

    picks = [(s, k, True) for s in range(1, strata) for k in order]
    picks += [(s, k, False) for s in range(strata) for k in order]
    rest = dict(zip(picks, rest_of_ratings(ratings, picks, rows)))
    rest.update({(0, k, True): t for k, t in zip(order, sends)})
    rates = {}
    for s in range(strata):
        for k in order:
            got = move(rest[s, k, True], 0, lambda i: i ^ 1)
            if s == 0 and k == order[0]:
                got, far_wide = got[:rows], got[rows:]
            rates[s, k] = (rest[s, k, False], got)

    for s in range(strata):
        if s:
            users_bf = users.astype(BF)
            shards = {0: users_bf}
            for k in range(1, group):
                shards[k] = move(users_bf, 0, lambda i: (i - 2 * k) % n)
            items_bf = items.astype(BF)
            near = move(items_bf, s, lambda i: i)
            far = move(items_bf, s, lambda i: i ^ 1)
        block = jax.ShapeDtypeStruct
        *parts, g_near = tile_call(
            functools.partial(near_kernel, group, s * tiles, side),
            group,
            [shards[k] for k in range(group)]
            + [rates[s, k][0] for k in range(group)]
            + [near, wide],
            (block((rows, rank), F32),) * group + (block((cols, rank), BF if s else F32),),
        )
        if s:
            g_near = move(g_near, -s, lambda i: i)
        user_shares = []
        carry = []
        for k in order:
            part, g_far = tile_call(
                functools.partial(far_kernel, k, s * tiles, side),
                1,
                [shards[k], far, rates[s, k][1], far_wide, parts[k]] + carry,
                (
                    block((rows, rank), BF if k else F32),
                    block((cols, rank), BF if k == order[-1] else F32),
                ),
            )
            carry = [g_far]
            if k:
                part = move(part, 0, lambda i: (i + 2 * k) % n)
            user_shares.append(part)
        g_far = move(g_far, -s, lambda i: i ^ 1)
        if s == strata - 1:
            users = last_update(users, user_accum, *user_shares)
            items = last_update(items, item_accum, g_near, g_far)
        else:
            user_grad = sum((t.astype(F32) for t in user_shares), 0.1 * users)
            item_grad = sum((t.astype(F32) for t in (g_near, g_far)), 0.1 * items)
            users, user_accum = adagrad(users, user_accum, user_grad)
            items, item_accum = adagrad(items, item_accum, item_grad)
    return (users, items)


def solution(mesh):
    rows = P(("user", "item"), None)
    blocks = P(None, "user", "item")

    return jax.shard_map(
        body,
        mesh=mesh,
        in_specs=(rows, rows, rows, rows, blocks, blocks),
        out_specs=(rows, rows),
        check_vma=False,
    )
```

```python
import functools

import jax
import jax.numpy as jnp
from jax import lax
from jax.experimental import pallas as pl
from jax.experimental.pallas import tpu as pltpu
from jax.sharding import PartitionSpec as P


BF = jnp.bfloat16
F32 = jnp.float32
SMALL = pltpu.CompilerParams(vmem_limit_bytes=16 << 20)


def adagrad(param, accum, grad):
    accum = accum + grad * grad
    return (param - 0.25 * grad / (jnp.sqrt(accum) + 1e-06), accum)


def move(array, by_user, item_map):
    n_user, n_item = lax.axis_size("user"), lax.axis_size("item")
    if by_user == 0:
        return lax.ppermute(array, "item", [(z, item_map(z)) for z in range(n_item)])
    pairs = [
        (u * n_item + z, (u + by_user) % n_user * n_item + item_map(z))
        for u in range(n_user)
        for z in range(n_item)
    ]
    return lax.ppermute(array, ("user", "item"), pairs)


def dot(a, b, ca, cb):
    return lax.dot_general(a, b, (((ca,), (cb,)), ((), ())), preferred_element_type=F32)


def tile_errors(k, first_tile, side, u, items, rates, seen):
    rows = u.shape[0]
    shard = lax.rem(lax.axis_index("item") + 2 * k, lax.axis_size("item"))
    chunk = min(rows, side)
    tiles, cols = seen.shape
    masks = seen[...].astype(F32)
    at = lax.broadcasted_iota(jnp.int32, (tiles, cols), 0)
    out = []
    for t in range(0, rows, chunk):
        tile = first_tile + (shard * rows + t) // side
        row = jnp.sum(jnp.where(at == tile, masks, 0.0), axis=0, keepdims=True)
        here = pl.ds(t, chunk)
        logits = dot(u[here, :], items[...], 1, 1)
        out.append((row * (jax.nn.sigmoid(logits) - rates[here, :].astype(F32))).astype(BF))
    return jnp.concatenate(out, axis=0) if len(out) > 1 else out[0]


def near_kernel(group, first_tile, side, *refs):
    shards, rates = refs[:group], refs[group : 2 * group]
    near, seen = refs[2 * group : 2 * group + 2]
    parts, grad = refs[2 * group + 2 : -1], refs[-1]
    total = None
    for k in range(group):
        errors = tile_errors(k, first_tile, side, shards[k], near, rates[k], seen)
        parts[k][...] = dot(errors, near[...], 1, 0)
        share = dot(errors, shards[k][...], 0, 0)
        total = share if total is None else total + share
    grad[...] = total.astype(grad.dtype)


def far_kernel(k, first_tile, side, *refs):
    u, far, rates, seen, part_in = refs[:5]
    carried, (part, grad) = refs[5:-2], refs[-2:]
    errors = tile_errors(k, first_tile, side, u, far, rates, seen)
    if k:
        part[...] = (part_in[...] + dot(errors, far[...], 1, 0)).astype(part.dtype)
    else:
        part[...] = errors
    share = dot(errors, u[...], 0, 0)
    for before in carried:
        share = share + before[...]
    grad[...] = share.astype(grad.dtype)


def tile_call(kernel, tiles, operands, out_shape):
    rows, rank = operands[0].shape
    cols = out_shape[-1].shape[0]
    spec = pl.BlockSpec(memory_space=pltpu.VMEM)
    return pl.pallas_call(
        kernel,
        out_shape=out_shape,
        in_specs=[spec] * len(operands),
        out_specs=(spec,) * len(out_shape),
        compiler_params=SMALL,
        cost_estimate=pl.CostEstimate(
            flops=6 * tiles * rows * cols * rank,
            bytes_accessed=0,
            transcendentals=2 * tiles * rows * cols,
        ),
    )(*operands)


def fetch(sources, buffers, sems):
    copies = [
        pltpu.make_async_copy(src, buf, sems.at[i])
        for i, (src, buf) in enumerate(zip(sources, buffers))
    ]
    for copy in copies:
        copy.start()
    return copies


def share(ratings, s, first, k, rows, n):
    at = pl.multiple_of(lax.rem(first + 2 * k, n) * rows, rows)
    return ratings.at[s, pl.ds(at, rows), :]


def rows_kernel(*refs):
    count = (len(refs) - 1) // 3
    sources, outs, bufs, sems = refs[:count], refs[count : 2 * count], refs[2 * count : -1], refs[-1]
    for copy, buf, out in zip(fetch(sources, bufs, sems), bufs, outs):
        copy.wait()
        out[...] = buf[...].astype(BF)


def first_rows(*arrays):
    return pl.pallas_call(
        rows_kernel,
        out_shape=tuple(jax.ShapeDtypeStruct(a.shape, BF) for a in arrays),
        in_specs=[pl.BlockSpec(memory_space=pltpu.HBM)] * len(arrays),
        out_specs=(pl.BlockSpec(memory_space=pltpu.VMEM),) * len(arrays),
        scratch_shapes=[pltpu.VMEM(a.shape, a.dtype) for a in arrays]
        + [pltpu.SemaphoreType.DMA((len(arrays),))],
        compiler_params=SMALL,
        name="first_rows",
    )(*(pltpu.with_memory_space_constraint(a, pltpu.HBM) for a in arrays))


def first_kernel(group, rows, side, *refs):
    ratings, masks, wide = refs[:3]
    sent = refs[3 : 3 + group]
    scratch = refs[3 + group :]
    n = lax.axis_size("item")
    other = lax.axis_index("item") ^ 1
    order = list(range(1, group)) + [0]
    sources = [masks] + [share(ratings, 0, other, k, rows, n) for k in order]
    copies = fetch(sources, scratch[:-1], scratch[-1])
    copies[0].wait()
    strata, across, tiles = masks.shape
    eye = lax.broadcasted_iota(jnp.int32, (tiles, tiles), 0) == lax.broadcasted_iota(
        jnp.int32, (tiles, tiles), 1
    )
    for s in range(strata):
        band = scratch[0][s].astype(F32)
        parts = []
        for c in range(across):
            spread = jnp.where(eye, jnp.broadcast_to(band[c : c + 1], (tiles, tiles)), 0.0)
            parts.append(jnp.broadcast_to(jnp.sum(spread, axis=1, keepdims=True), (tiles, side)))
        wide[pl.ds(s * tiles, tiles), :] = jnp.concatenate(parts, axis=1)
    for i, out in enumerate(sent):
        copies[1 + i].wait()
        out[pl.ds(0, rows), :] = scratch[1 + i][...].astype(F32).astype(BF)
    sent[0][pl.ds(rows, tiles), :] = wide[pl.ds(0, tiles), :].astype(BF)


def first_sends(ratings, tile_mask, rows, group, side):
    cols = ratings.shape[2]
    masks = tile_mask.transpose(0, 2, 1)
    wide = (tile_mask.shape[0] * tile_mask.shape[1], cols)
    vmem = pl.BlockSpec(memory_space=pltpu.VMEM)
    out_shape = [
        jax.ShapeDtypeStruct(wide, F32),
        jax.ShapeDtypeStruct((rows + tile_mask.shape[1], cols), BF),
    ] + [jax.ShapeDtypeStruct((rows, cols), BF)] * (group - 1)
    return pl.pallas_call(
        functools.partial(first_kernel, group, rows, side),
        out_shape=tuple(out_shape),
        in_specs=[pl.BlockSpec(memory_space=pltpu.HBM)] * 2,
        out_specs=(vmem,) * len(out_shape),
        scratch_shapes=[pltpu.VMEM(masks.shape, jnp.int32)]
        + [pltpu.VMEM((rows, cols), jnp.int32)] * group
        + [pltpu.SemaphoreType.DMA((1 + group,))],
        compiler_params=SMALL,
        name="first_sends",
    )(*(pltpu.with_memory_space_constraint(a, pltpu.HBM) for a in (ratings, masks)))


def rest_kernel(picks, rows, ratings, *refs):
    outs, bufs, sems = refs[: len(picks)], refs[len(picks) : -1], refs[-1]
    n = lax.axis_size("item")
    z = lax.axis_index("item")
    copies = fetch(
        [share(ratings, s, z ^ 1 if away else z, k, rows, n) for s, k, away in picks], bufs, sems
    )
    for copy, buf, out in zip(copies, bufs, outs):
        copy.wait()
        out[...] = buf[...].astype(F32).astype(BF)


def rest_of_ratings(ratings, picks, rows):
    cols = ratings.shape[2]
    vmem = pl.BlockSpec(memory_space=pltpu.VMEM)
    return pl.pallas_call(
        functools.partial(rest_kernel, picks, rows),
        out_shape=(jax.ShapeDtypeStruct((rows, cols), BF),) * len(picks),
        in_specs=[pl.BlockSpec(memory_space=pltpu.HBM)],
        out_specs=(vmem,) * len(picks),
        scratch_shapes=[pltpu.VMEM((rows, cols), jnp.int32)] * len(picks)
        + [pltpu.SemaphoreType.DMA((len(picks),))],
        compiler_params=SMALL,
        name="rest_of_ratings",
    )(pltpu.with_memory_space_constraint(ratings, pltpu.HBM))


def last_kernel(count, *refs):
    param, accum = refs[:2]
    grads, out, buf, sems = refs[2:-3], refs[-3], refs[-2], refs[-1]
    band = param.shape[0] // count
    copies = []
    for i in range(count):
        here = pl.ds(i * band, band)
        old = param[here, :]
        grad = 0.1 * old
        for share in grads:
            grad = grad + share[here, :].astype(F32)
        buf[here, :] = adagrad(old, accum[here, :], grad)[0]
        copies.append(pltpu.make_async_copy(buf.at[here, :], out.at[here, :], sems.at[i]))
        copies[-1].start()
    for copy in copies:
        copy.wait()


def last_update(param, accum, *grads):
    count = 4
    vmem = pl.BlockSpec(memory_space=pltpu.VMEM)
    return pl.pallas_call(
        functools.partial(last_kernel, count),
        out_shape=jax.ShapeDtypeStruct(param.shape, F32),
        in_specs=[vmem] * (2 + len(grads)),
        out_specs=pl.BlockSpec(memory_space=pltpu.HBM),
        scratch_shapes=[pltpu.VMEM(param.shape, F32), pltpu.SemaphoreType.DMA((count,))],
        compiler_params=SMALL,
        name="last_update",
    )(param, accum, *grads)


def body(users, user_accum, items, item_accum, ratings, tile_mask):
    strata, block_users, cols = ratings.shape
    rows, rank = users.shape
    n = lax.axis_size("item")
    group = n // 2
    tiles = tile_mask.shape[1]
    side = block_users // tiles
    order = list(range(1, group)) + [0]

    first_items, first_users = first_rows(items, users)
    wide, *sends = first_sends(ratings, tile_mask, rows, group, side)
    shards = {0: first_users}
    for k in range(1, group):
        shards[k] = move(first_users, 0, lambda i: (i - 2 * k) % n)
    near, far = first_items, move(first_items, 0, lambda i: i ^ 1)

    picks = [(s, k, True) for s in range(1, strata) for k in order]
    picks += [(s, k, False) for s in range(strata) for k in order]
    rest = dict(zip(picks, rest_of_ratings(ratings, picks, rows)))
    rest.update({(0, k, True): t for k, t in zip(order, sends)})
    rates, far_wide = {}, {}
    for s in range(strata):
        for k in order:
            sent = rest[s, k, True]
            if s and k == order[0]:
                sent = jnp.concatenate((sent, wide[s * tiles : (s + 1) * tiles].astype(BF)))
            got = move(sent, 0, lambda i: i ^ 1)
            if k == order[0]:
                got, far_wide[s] = got[:rows], got[rows:]
            rates[s, k] = (rest[s, k, False], got)

    for s in range(strata):
        if s:
            users_bf = users.astype(BF)
            shards = {0: users_bf}
            for k in range(1, group):
                shards[k] = move(users_bf, 0, lambda i: (i - 2 * k) % n)
            items_bf = items.astype(BF)
            near = move(items_bf, s, lambda i: i)
            far = move(items_bf, s, lambda i: i ^ 1)
        block = jax.ShapeDtypeStruct
        *parts, g_near = tile_call(
            functools.partial(near_kernel, group, s * tiles, side),
            group,
            [shards[k] for k in range(group)]
            + [rates[s, k][0] for k in range(group)]
            + [near, wide],
            (block((rows, rank), F32),) * group + (block((cols, rank), BF if s else F32),),
        )
        if s:
            g_near = move(g_near, -s, lambda i: i)
        user_shares = []
        carry = []
        for k in order:
            part, g_far = tile_call(
                functools.partial(far_kernel, k, 0, side),
                1,
                [shards[k], far, rates[s, k][1], far_wide[s], parts[k]] + carry,
                (
                    block((rows, rank if k else cols), BF),
                    block((cols, rank), BF if k == order[-1] else F32),
                ),
            )
            carry = [g_far]
            if k:
                part = move(part, 0, lambda i: (i + 2 * k) % n)
            else:
                part = parts[k] + dot(part, far, 1, 0)
            user_shares.append(part)
        g_far = move(g_far, -s, lambda i: i ^ 1)
        if s == strata - 1:
            users = last_update(users, user_accum, *user_shares)
            items = last_update(items, item_accum, g_near, g_far)
        else:
            user_grad = sum((t.astype(F32) for t in user_shares), 0.1 * users)
            item_grad = sum((t.astype(F32) for t in (g_near, g_far)), 0.1 * items)
            users, user_accum = adagrad(users, user_accum, user_grad)
            items, item_accum = adagrad(items, item_accum, item_grad)
    return (users, items)


def solution(mesh):
    rows = P(("user", "item"), None)
    blocks = P(None, "user", "item")

    return jax.shard_map(
        body,
        mesh=mesh,
        in_specs=(rows, rows, rows, rows, blocks, blocks),
        out_specs=(rows, rows),
        check_vma=False,
    )
```
